32 devices in a mesh: dp: 16 (over z, y, x), mp: 2 (over core).
Axes of the slice: x: 2, y: 2, z: 4, core: 2. Of those that a mesh axis runs over, the one named last changes fastest.
Arguments:
- images: bfloat16 [32768, 384], P('dp'), may hold values from -6 to 6
- means: float32 [8192, 384], P(('mp', 'dp')), may hold values from -0.6 to 0.6
- precisions: float32 [8192, 384], P(('mp', 'dp')), may hold values from 0.5 to 2
- logits: float32 [8192], replicated, may hold values from -6 to 6
Outputs:
- new_means: float32 [8192, 384], P(('mp', 'dp'))
- new_variances: float32 [8192, 384], P(('mp', 'dp'))
- new_log_weights: float32 [8192], P(('mp', 'dp'))
- log_likelihood: float32 [32768], P('dp')
The draws below stay inside these ranges and needn't reach their ends.
All inputs are finite; a program needn't handle non-finite values.
Results may differ from the reference program's by a relative error of at most 0.0039.
The reference program's roundings to bfloat16 on the way (of `squares`, `prec_b`, `scaled` and `shares`) count: a program that leaves them out, or rounds other values in their place, can miss the bound.
Values may be sent and summed in bfloat16 or wider, within the bound.
A program may use at most 128 MiB of HBM per device.

```python
import math
import jax
import jax.numpy as jnp
from jax import lax

D = 384
K = 8192
TOK_DEV = 2048
N = 32768
N_DP = 16


def block_levels(key, extent, shards, least, largest):
    loudness = 1.0
    for dim, parts in shards:
        steps = jax.random.uniform(jax.random.fold_in(jax.random.fold_in(key, 6), dim), (parts,), jnp.float32, least / len(shards), largest / len(shards))
        loudness = loudness * jnp.repeat(jnp.exp(steps), extent[dim] // parts).reshape((-1,) + (1,) * (len(extent) - 1 - dim))
    return loudness


def noise(rng, extent, scale, reach, cuts=(), dtype=jnp.bfloat16):
    array = jax.random.normal(rng, extent, jnp.float32) * scale
    if len(cuts) > 0:
        array = block_levels(rng, extent, cuts, -0.22, 0.18) * array
    return jnp.clip(array, min=-reach, max=reach).astype(dtype)


def setup_inputs(seed: int = 0) -> dict:
    key_list = jax.random.split(jax.random.key(seed), 5)
    return {
        "images": noise(key_list[0], (N, D), 1.0, 6.0, ((0, 16),)),
        "means": noise(key_list[1], (K, D), 0.1, 0.6, ((0, 32),), jnp.float32),
        "precisions": jnp.clip(jnp.exp(math.log(2.0) - 1.3862944 * jax.random.uniform(key_list[2], (K, D), jnp.float32) ** block_levels(key_list[2], (K, D), ((0, 32),), -0.2, 0.2)), 0.5, 2.0),
        "logits": noise(key_list[3], (K,), 1.0, 6.0, (), jnp.float32),
    }


def matmul_t(left, right):
    return jnp.dot(left.astype(jnp.float32), right.astype(jnp.float32).T, preferred_element_type=jnp.float32, precision=lax.Precision.HIGHEST)


def reference(images, means, precisions, logits):
    prec_b = precisions.astype(jnp.bfloat16)
    scaled = (means * precisions).astype(jnp.bfloat16)
    offset = logits + 0.5 * jnp.sum(jnp.log(precisions) - means * means * precisions, axis=1) - 0.5 * D * math.log(2.0 * math.pi)
    logit_peak = jnp.max(logits)
    logit_total = logit_peak + jnp.log(jnp.sum(jnp.exp(logits - logit_peak)))
    blocks = images.reshape(N_DP, TOK_DEV, D)

    def update(running, image_block):
        counts, moments = running
        squares = (image_block.astype(jnp.float32) * image_block.astype(jnp.float32)).astype(jnp.bfloat16)
        scores = -0.5 * matmul_t(squares, prec_b) + matmul_t(image_block, scaled) + offset[None, :]
        row_peak = jnp.max(scores, axis=1)
        row_total = row_peak + jnp.log(jnp.sum(jnp.exp(scores - row_peak[:, None]), axis=1))
        shares = jnp.exp(scores - row_total[:, None]).astype(jnp.bfloat16)
        features = jnp.concatenate([image_block, squares], axis=1)
        counts = counts + jnp.sum(shares.astype(jnp.float32), axis=0)
        moments = moments + jnp.dot(shares.astype(jnp.float32).T, features.astype(jnp.float32), preferred_element_type=jnp.float32, precision=lax.Precision.HIGHEST)
        return (counts, moments), row_total - logit_total

    start = (jnp.zeros((K,), jnp.float32), jnp.zeros((K, 2 * D), jnp.float32))
    (counts, moments), likely = lax.scan(update, start, blocks)
    denominator = counts + 1.0
    new_means = (moments[:, :D] + means) / denominator[:, None]
    second = (moments[:, D:] + 1.0 / precisions + means * means) / denominator[:, None]
    new_variances = second - new_means * new_means
    new_log_weights = jnp.log(denominator) - jnp.log(jnp.float32(N + K))
    return new_means, new_variances, new_log_weights, likely.reshape(-1)
```

```python
import functools
import math

import jax
import jax.numpy as jnp
from jax import lax
from jax.experimental import pallas as pl
from jax.experimental.pallas import tpu as pltpu
from jax.sharding import Mesh, PartitionSpec as P

MESH = pl.DeviceIdType.MESH
SQUARE = 4
CHUNK = 512
F32 = jnp.float32
BF16 = jnp.bfloat16
VMEM_LIMIT = 60 * 1024 * 1024


def remote(src, dst, send, recv, device):
    return pltpu.make_async_remote_copy(
        src_ref=src, dst_ref=dst, send_sem=send, recv_sem=recv, device_id=device, device_id_type=MESH
    )


def gather_kernel(n_ca, img_ref, w_ref, off_ref, imgs_ref, wall_ref, offall_ref, stage,
                  loc, isend, irecv, wsend, wrecv, osend, orecv):
    a, b, m = lax.axis_index("ca"), lax.axis_index("ib"), lax.axis_index("mp")
    core = lax.rem(m, 2)
    partner = m + 1 - 2 * core
    bx = b + 1 - 2 * lax.rem(b, 2)
    by = lax.rem(b + 2, 4)
    bd = lax.rem(bx + 2, 4)
    to_x, to_y, to_p = (a, bx, m), (a, by, m), (a, b, partner)
    half_rows = img_ref.shape[0] // 2
    half = pl.ds(pl.multiple_of(core * half_rows, half_rows), half_rows)

    barrier = pltpu.get_barrier_semaphore()
    for dev in (to_x, to_y, to_p):
        pl.semaphore_signal(barrier, inc=1, device_id=dev, device_id_type=MESH)

    @pl.when(a > 0)
    def _():
        pl.semaphore_signal(barrier, inc=1, device_id=(a - 1, b, m), device_id_type=MESH)

    @pl.when(a < n_ca - 1)
    def _():
        pl.semaphore_signal(barrier, inc=1, device_id=(a + 1, b, m), device_id_type=MESH)

    own_in = pltpu.make_async_copy(img_ref, stage, loc.at[0])
    own_in.start()
    own_w = pltpu.make_async_copy(w_ref, wall_ref.at[a], loc.at[1])
    own_w.start()
    own_o = pltpu.make_async_copy(off_ref, offall_ref.at[a], loc.at[2])
    own_o.start()

    ends = (a == 0).astype(jnp.int32) + (a == n_ca - 1).astype(jnp.int32)
    pl.semaphore_wait(barrier, 5 - ends)

    def shard(i, src_own=False):
        src = img_ref.at[half] if src_own else imgs_ref.at[i, half]
        return src, imgs_ref.at[i, half]

    def img_copy(k, i, dev, src_own=False):
        src, dst = shard(i, src_own)
        return remote(src, dst, isend.at[k], irecv.at[k], dev)

    send_x = img_copy(0, b, to_x, True)
    send_y = img_copy(1, b, to_y, True)
    send_x.start()
    send_y.start()

    def chain(direction, s):
        blk = a - s if direction == 0 else a + s
        blk_ok = (blk >= 0) if direction == 0 else (blk < n_ca)
        nbr_ok = (a < n_ca - 1) if direction == 0 else (a > 0)
        nbr = a + 1 if direction == 0 else a - 1
        blk_c = jnp.clip(blk, 0, n_ca - 1)
        src_w = w_ref if s == 0 else wall_ref.at[blk_c]
        src_o = off_ref if s == 0 else offall_ref.at[blk_c]
        dev = (nbr, b, m)
        cw = remote(src_w, wall_ref.at[blk_c], wsend.at[direction, s], wrecv.at[direction, s], dev)
        co = remote(src_o, offall_ref.at[blk_c], osend.at[direction, s], orecv.at[direction, s], dev)
        return jnp.logical_and(blk_ok, nbr_ok), cw, co

    def chain_recv(direction, s):
        blk = a - 1 - s if direction == 0 else a + 1 + s
        ok = (blk >= 0) if direction == 0 else (blk < n_ca)
        blk_c = jnp.clip(blk, 0, n_ca - 1)
        nbr = jnp.clip(a + 1 if direction == 0 else a - 1, 0, n_ca - 1)
        dev = (nbr, b, m)
        cw = remote(w_ref, wall_ref.at[blk_c], wsend.at[direction, s], wrecv.at[direction, s], dev)
        co = remote(off_ref, offall_ref.at[blk_c], osend.at[direction, s], orecv.at[direction, s], dev)
        return ok, cw, co

    def start_chain(s):
        for d in (0, 1):
            ok, cw, co = chain(d, s)

            @pl.when(ok)
            def _():
                cw.start()
                co.start()

    def wait_chain(s):
        for d in (0, 1):
            ok, cw, co = chain_recv(d, s)

            @pl.when(ok)
            def _():
                cw.wait_recv()
                co.wait_recv()

    start_chain(0)
    own_in.wait()
    own_out = pltpu.make_async_copy(stage, imgs_ref.at[b], loc.at[0])
    own_out.start()
    wait_chain(0)
    if n_ca > 2:
        start_chain(1)
    send_x.wait_recv()
    pass_x = img_copy(3, bx, to_p)
    pass_x.start()

    @pl.when(core == 0)
    def _():
        img_copy(2, bx, to_y).start()

    send_y.wait_recv()
    pass_y = img_copy(4, by, to_p)
    pass_y.start()

    @pl.when(core == 1)
    def _():
        img_copy(2, by, to_x).start()

    for s in range(1, n_ca - 1):
        wait_chain(s)
        if s + 1 < n_ca - 1:
            start_chain(s + 1)
    relay = img_copy(2, bd, to_x)
    relay.wait_recv()
    pass_d = img_copy(5, bd, to_p)
    pass_d.start()
    for c in (pass_x, pass_y, pass_d):
        c.wait()
    for c in (send_x, send_y, relay):
        c.wait_send()
    for s in range(n_ca - 1):
        for d in (0, 1):
            ok, cw, co = chain(d, s)

            @pl.when(ok)
            def _():
                cw.wait_send()
                co.wait_send()
    own_out.wait()
    own_w.wait()
    own_o.wait()


def gather(images, w, off, n_ca):
    t, d = images.shape
    any_spec = pl.BlockSpec(memory_space=pl.ANY)
    vmem = pl.BlockSpec(memory_space=pltpu.VMEM)
    dma = pltpu.SemaphoreType.DMA
    return pl.pallas_call(
        functools.partial(gather_kernel, n_ca),
        out_shape=(
            jax.ShapeDtypeStruct((SQUARE, t, d), BF16),
            jax.ShapeDtypeStruct((n_ca,) + w.shape, BF16),
            jax.ShapeDtypeStruct((n_ca,) + off.shape, F32),
        ),
        in_specs=[any_spec, vmem, vmem],
        out_specs=(any_spec, vmem, vmem),
        scratch_shapes=[
            pltpu.VMEM((t, d), BF16),
            dma((3,)),
            dma((6,)),
            dma((6,)),
            dma((2, n_ca - 1)),
            dma((2, n_ca - 1)),
            dma((2, n_ca - 1)),
            dma((2, n_ca - 1)),
        ],
        compiler_params=pltpu.CompilerParams(
            collective_id=0, has_side_effects=True, vmem_limit_bytes=VMEM_LIMIT
        ),
        name="gather",
    )(images, w, off)


def features(x):
    wide = x.astype(F32)
    return jnp.concatenate([(wide * wide).astype(BF16), x], axis=1)


def score_kernel(x_ref, w_ref, off_ref, e_ref, peak_ref, lse_ref):
    feats = features(x_ref[...])
    s = lax.dot_general(w_ref[...], feats, (((1,), (1,)), ((), ())), preferred_element_type=F32)
    s = s + off_ref[...]
    peak = jnp.max(s, axis=0, keepdims=True)
    e = jnp.exp(s - peak)
    e_ref[...] = e
    peak_ref[...] = peak
    lse_ref[...] = peak + jnp.log(jnp.sum(e, axis=0, keepdims=True))


def score(x, w, off):
    rows, d = x.shape
    k = w.shape[0]
    n = min(CHUNK, rows)
    whole = lambda i: (0, 0)
    return pl.pallas_call(
        score_kernel,
        grid=(rows // n,),
        out_shape=(
            jax.ShapeDtypeStruct((k, rows), F32),
            jax.ShapeDtypeStruct((1, rows), F32),
            jax.ShapeDtypeStruct((1, rows), F32),
        ),
        in_specs=[
            pl.BlockSpec((n, d), lambda i: (i, 0)),
            pl.BlockSpec((k, 2 * d), whole),
            pl.BlockSpec((k, 1), whole),
        ],
        out_specs=(
            pl.BlockSpec((k, n), lambda i: (0, i)),
            pl.BlockSpec((1, n), lambda i: (0, i)),
            pl.BlockSpec((1, n), lambda i: (0, i)),
        ),
        compiler_params=pltpu.CompilerParams(vmem_limit_bytes=VMEM_LIMIT),
        name="score",
    )(x, w, off)


def lse_kernel(n_mp, lse_ref, peak_ref, logits_ref, factor_ref, like_ref, buf, send, recv):
    a, b, m = lax.axis_index("ca"), lax.axis_index("ib"), lax.axis_index("mp")
    n = SQUARE * n_mp
    me = b * n_mp + m

    def device(k):
        p = lax.rem(me + k, n)
        return (a, p // n_mp, lax.rem(p, n_mp))

    barrier = pltpu.get_barrier_semaphore()

    @pl.loop(1, n)
    def _(k):
        pl.semaphore_signal(barrier, inc=1, device_id=device(k), device_id_type=MESH)

    pl.semaphore_wait(barrier, n - 1)

    def copy(k):
        return remote(lse_ref, buf.at[k], send.at[k], recv.at[k], device(k))

    @pl.loop(1, n)
    def _(k):
        copy(k).start()

    logits = logits_ref[...]
    top = jnp.max(logits, axis=1, keepdims=True)
    logit_total = top + jnp.log(jnp.sum(jnp.exp(logits - top), axis=1, keepdims=True))

    @pl.loop(1, n)
    def _(k):
        copy(k).wait()

    own = lse_ref[...]
    high = lax.fori_loop(1, n, lambda k, h: jnp.maximum(h, buf[k]), own)
    total = lax.fori_loop(1, n, lambda k, t: t + jnp.exp(buf[k] - high), jnp.exp(own - high))
    row_total = high + jnp.log(total)
    factor_ref[...] = jnp.exp(peak_ref[...] - row_total)
    like_ref[...] = row_total - logit_total


def combine(lse, peak, logits, n_mp):
    n = SQUARE * n_mp
    vmem = pl.BlockSpec(memory_space=pltpu.VMEM)
    return pl.pallas_call(
        functools.partial(lse_kernel, n_mp),
        out_shape=(jax.ShapeDtypeStruct(lse.shape, F32),) * 2,
        in_specs=[vmem] * 3,
        out_specs=(vmem,) * 2,
        scratch_shapes=[
            pltpu.VMEM((n,) + lse.shape, F32),
            pltpu.SemaphoreType.DMA((n,)),
            pltpu.SemaphoreType.DMA((n,)),
        ],
        compiler_params=pltpu.CompilerParams(collective_id=1, has_side_effects=True),
        name="combine",
    )(lse, peak, logits[None, :])


def moment_kernel(x_ref, e_ref, factor_ref, mom_ref, cnt_ref, acc, cacc):
    i = pl.program_id(0)

    @pl.when(i == 0)
    def _():
        acc[...] = jnp.zeros_like(acc)
        cacc[...] = jnp.zeros_like(cacc)

    feats = features(x_ref[...])
    shares = (e_ref[...] * factor_ref[...]).astype(BF16)
    wide = shares.astype(F32)
    part = cacc[...]
    for j in range(wide.shape[1] // 128):
        part = part + wide[:, j * 128:(j + 1) * 128]
    cacc[...] = part
    acc[...] += jnp.dot(shares, feats, preferred_element_type=F32)

    @pl.when(i == pl.num_programs(0) - 1)
    def _():
        mom_ref[...] = acc[...].astype(BF16)
        cnt_ref[...] = jnp.sum(cacc[...], axis=1, keepdims=True)


def moment(x, e, factor):
    rows, d = x.shape
    k = e.shape[0]
    n = min(CHUNK, rows)
    return pl.pallas_call(
        moment_kernel,
        grid=(rows // n,),
        out_shape=(
            jax.ShapeDtypeStruct((k, 2 * d), BF16),
            jax.ShapeDtypeStruct((k, 1), F32),
        ),
        in_specs=[
            pl.BlockSpec((n, d), lambda i: (i, 0)),
            pl.BlockSpec((k, n), lambda i: (0, i)),
            pl.BlockSpec((1, n), lambda i: (0, i)),
        ],
        out_specs=(
            pl.BlockSpec((k, 2 * d), lambda i: (0, 0)),
            pl.BlockSpec((k, 1), lambda i: (0, 0)),
        ),
        scratch_shapes=[pltpu.VMEM((k, 2 * d), F32), pltpu.VMEM((k, 128), F32)],
        compiler_params=pltpu.CompilerParams(vmem_limit_bytes=VMEM_LIMIT),
        name="moment",
    )(x, e, factor)


def scatter_kernel(n_ca, mom_ref, cnt_ref, out_ref, cout_ref, loc, msend, mrecv, csend, crecv):
    a, b, m = lax.axis_index("ca"), lax.axis_index("ib"), lax.axis_index("mp")
    barrier = pltpu.get_barrier_semaphore()

    def other(k):
        return lax.rem(a + k, n_ca)

    @pl.loop(1, n_ca)
    def _(k):
        pl.semaphore_signal(barrier, inc=1, device_id=(other(k), b, m), device_id_type=MESH)

    own_m = pltpu.make_async_copy(mom_ref.at[a], out_ref.at[0], loc.at[0])
    own_c = pltpu.make_async_copy(cnt_ref.at[a], cout_ref.at[0], loc.at[1])
    own_m.start()
    own_c.start()
    pl.semaphore_wait(barrier, n_ca - 1)

    def copies(k):
        p = other(k)
        dev = (p, b, m)
        return (
            remote(cnt_ref.at[p], cout_ref.at[k], csend.at[k], crecv.at[k], dev),
            remote(mom_ref.at[p], out_ref.at[k], msend.at[k], mrecv.at[k], dev),
        )

    @pl.loop(1, n_ca)
    def _(k):
        for c in copies(k):
            c.start()

    @pl.loop(1, n_ca)
    def _(k):
        for c in copies(k):
            c.wait()

    own_m.wait()
    own_c.wait()


def scatter(mom, cnt, n_ca):
    vmem = pl.BlockSpec(memory_space=pltpu.VMEM)
    dma = pltpu.SemaphoreType.DMA
    return pl.pallas_call(
        functools.partial(scatter_kernel, n_ca),
        out_shape=(jax.ShapeDtypeStruct(mom.shape, BF16), jax.ShapeDtypeStruct(cnt.shape, F32)),
        in_specs=[vmem] * 2,
        out_specs=(vmem,) * 2,
        scratch_shapes=[dma((2,)), dma((n_ca,)), dma((n_ca,)), dma((n_ca,)), dma((n_ca,))],
        compiler_params=pltpu.CompilerParams(
            collective_id=2, has_side_effects=True, vmem_limit_bytes=VMEM_LIMIT
        ),
        name="scatter",
    )(mom, cnt)


def body(n_ca, n_mp, images, means, precisions, logits):
    t, d = images.shape
    r = means.shape[0]
    a, b, m = lax.axis_index("ca"), lax.axis_index("ib"), lax.axis_index("mp")
    own_logits = lax.dynamic_slice_in_dim(logits, ((m * n_ca + a) * SQUARE + b) * r, r)
    prec_b = precisions.astype(BF16)
    w = jnp.concatenate([-0.5 * prec_b, (means * precisions).astype(BF16)], axis=1)
    off = (
        own_logits
        + 0.5 * jnp.sum(jnp.log(precisions) - means * means * precisions, axis=1)
        - 0.5 * d * math.log(2.0 * math.pi)
    )
    imgs, w_all, off_all = gather(images, w, off[None, :], n_ca)
    x = imgs.reshape(SQUARE * t, d)
    e, peak, lse = score(x, w_all.reshape(n_ca * r, 2 * d), off_all.reshape(n_ca * r, 1))
    factor, like = combine(lse, peak, logits, n_mp)
    log_likelihood = lax.dynamic_slice_in_dim(like[0], b * t, t)
    mom, cnt = moment(x, e, factor)
    mom, cnt = scatter(mom.reshape(n_ca, r, 2 * d), cnt.reshape(n_ca, 1, r), n_ca)
    own_moments = jnp.sum(mom.astype(F32), axis=0)
    denominator = jnp.sum(cnt, axis=0)[0] + 1.0
    new_means = (own_moments[:, d:] + means) / denominator[:, None]
    second = (own_moments[:, :d] + 1.0 / precisions + means * means) / denominator[:, None]
    new_variances = second - new_means * new_means
    total = t * n_ca * SQUARE + logits.shape[0]
    new_log_weights = jnp.log(denominator) - jnp.log(jnp.float32(total))
    return (new_means, new_variances, new_log_weights, log_likelihood)


def solution(mesh):
    n_dp, n_mp = mesh.shape["dp"], mesh.shape["mp"]
    n_ca = n_dp // SQUARE
    split = Mesh(mesh.devices.reshape(n_ca, SQUARE, n_mp), ("ca", "ib", "mp"))
    dp = ("ca", "ib")
    comp = ("mp", "ca", "ib")
    return jax.shard_map(
        functools.partial(body, n_ca, n_mp),
        mesh=split,
        in_specs=(P(dp, None), P(comp, None), P(comp, None), P()),
        out_specs=(P(comp, None), P(comp, None), P(comp), P(dp)),
        check_vma=False,
    )
```

```python
import functools
import math

import jax
import jax.numpy as jnp
from jax import lax
from jax.experimental import pallas as pl
from jax.experimental.pallas import tpu as pltpu
from jax.sharding import Mesh, PartitionSpec as P

MESH = pl.DeviceIdType.MESH
SQUARE = 4
CHUNK = 512
F32 = jnp.float32
BF16 = jnp.bfloat16
VMEM_LIMIT = 60 * 1024 * 1024


def remote(src, dst, send, recv, device):
    return pltpu.make_async_remote_copy(
        src_ref=src, dst_ref=dst, send_sem=send, recv_sem=recv, device_id=device, device_id_type=MESH
    )


def gather_kernel(n_ca, img_ref, w_ref, off_ref, imgs_ref, wall_ref, offall_ref, stage,
                  loc, isend, irecv, wsend, wrecv, osend, orecv):
    a, b, m = lax.axis_index("ca"), lax.axis_index("ib"), lax.axis_index("mp")
    core = lax.rem(m, 2)
    partner = m + 1 - 2 * core
    bx = b + 1 - 2 * lax.rem(b, 2)
    by = lax.rem(b + 2, 4)
    bd = lax.rem(bx + 2, 4)
    to_x, to_y, to_p = (a, bx, m), (a, by, m), (a, b, partner)
    half_rows = img_ref.shape[0] // 2
    half = pl.ds(pl.multiple_of(core * half_rows, half_rows), half_rows)

    barrier = pltpu.get_barrier_semaphore()
    for dev in (to_x, to_y, to_p):
        pl.semaphore_signal(barrier, inc=1, device_id=dev, device_id_type=MESH)

    @pl.when(a > 0)
    def _():
        pl.semaphore_signal(barrier, inc=1, device_id=(a - 1, b, m), device_id_type=MESH)

    @pl.when(a < n_ca - 1)
    def _():
        pl.semaphore_signal(barrier, inc=1, device_id=(a + 1, b, m), device_id_type=MESH)

    own_in = pltpu.make_async_copy(img_ref, stage, loc.at[0])
    own_in.start()
    own_w = pltpu.make_async_copy(w_ref, wall_ref.at[a], loc.at[1])
    own_w.start()
    own_o = pltpu.make_async_copy(off_ref, offall_ref.at[a], loc.at[2])
    own_o.start()

    ends = (a == 0).astype(jnp.int32) + (a == n_ca - 1).astype(jnp.int32)
    pl.semaphore_wait(barrier, 5 - ends)

    def shard(i, src_own=False):
        src = img_ref.at[half] if src_own else imgs_ref.at[i, half]
        return src, imgs_ref.at[i, half]

    def img_copy(k, i, dev, src_own=False):
        src, dst = shard(i, src_own)
        return remote(src, dst, isend.at[k], irecv.at[k], dev)

    send_x = img_copy(0, b, to_x, True)
    send_y = img_copy(1, b, to_y, True)
    send_x.start()
    send_y.start()

    def chain(direction, s):
        blk = a - s if direction == 0 else a + s
        blk_ok = (blk >= 0) if direction == 0 else (blk < n_ca)
        nbr_ok = (a < n_ca - 1) if direction == 0 else (a > 0)
        nbr = a + 1 if direction == 0 else a - 1
        blk_c = jnp.clip(blk, 0, n_ca - 1)
        src_w = w_ref if s == 0 else wall_ref.at[blk_c]
        src_o = off_ref if s == 0 else offall_ref.at[blk_c]
        dev = (nbr, b, m)
        cw = remote(src_w, wall_ref.at[blk_c], wsend.at[direction, s], wrecv.at[direction, s], dev)
        co = remote(src_o, offall_ref.at[blk_c], osend.at[direction, s], orecv.at[direction, s], dev)
        return jnp.logical_and(blk_ok, nbr_ok), cw, co

    def chain_recv(direction, s):
        blk = a - 1 - s if direction == 0 else a + 1 + s
        ok = (blk >= 0) if direction == 0 else (blk < n_ca)
        blk_c = jnp.clip(blk, 0, n_ca - 1)
        nbr = jnp.clip(a + 1 if direction == 0 else a - 1, 0, n_ca - 1)
        dev = (nbr, b, m)
        cw = remote(w_ref, wall_ref.at[blk_c], wsend.at[direction, s], wrecv.at[direction, s], dev)
        co = remote(off_ref, offall_ref.at[blk_c], osend.at[direction, s], orecv.at[direction, s], dev)
        return ok, cw, co

    def start_chain(s):
        for d in (0, 1):
            ok, cw, co = chain(d, s)

            @pl.when(ok)
            def _():
                cw.start()
                co.start()

    def wait_chain(s):
        for d in (0, 1):
            ok, cw, co = chain_recv(d, s)

            @pl.when(ok)
            def _():
                cw.wait_recv()
                co.wait_recv()

    start_chain(0)
    own_in.wait()
    own_out = pltpu.make_async_copy(stage, imgs_ref.at[b], loc.at[0])
    own_out.start()
    wait_chain(0)
    if n_ca > 2:
        start_chain(1)
    send_x.wait_recv()
    pass_x = img_copy(3, bx, to_p)
    pass_x.start()

    @pl.when(core == 0)
    def _():
        img_copy(2, bx, to_y).start()

    send_y.wait_recv()
    pass_y = img_copy(4, by, to_p)
    pass_y.start()

    @pl.when(core == 1)
    def _():
        img_copy(2, by, to_x).start()

    for s in range(1, n_ca - 1):
        wait_chain(s)
        if s + 1 < n_ca - 1:
            start_chain(s + 1)
    relay = img_copy(2, bd, to_x)
    relay.wait_recv()
    pass_d = img_copy(5, bd, to_p)
    pass_d.start()
    for c in (pass_x, pass_y, pass_d):
        c.wait()
    for c in (send_x, send_y, relay):
        c.wait_send()
    for s in range(n_ca - 1):
        for d in (0, 1):
            ok, cw, co = chain(d, s)

            @pl.when(ok)
            def _():
                cw.wait_send()
                co.wait_send()
    own_out.wait()
    own_w.wait()
    own_o.wait()


def gather(images, w, off, n_ca):
    t, d = images.shape
    any_spec = pl.BlockSpec(memory_space=pl.ANY)
    vmem = pl.BlockSpec(memory_space=pltpu.VMEM)
    dma = pltpu.SemaphoreType.DMA
    return pl.pallas_call(
        functools.partial(gather_kernel, n_ca),
        out_shape=(
            jax.ShapeDtypeStruct((SQUARE, t, d), BF16),
            jax.ShapeDtypeStruct((n_ca,) + w.shape, BF16),
            jax.ShapeDtypeStruct((n_ca,) + off.shape, F32),
        ),
        in_specs=[any_spec, vmem, vmem],
        out_specs=(any_spec, vmem, vmem),
        scratch_shapes=[
            pltpu.VMEM((t, d), BF16),
            dma((3,)),
            dma((6,)),
            dma((6,)),
            dma((2, n_ca - 1)),
            dma((2, n_ca - 1)),
            dma((2, n_ca - 1)),
            dma((2, n_ca - 1)),
        ],
        compiler_params=pltpu.CompilerParams(
            collective_id=0, has_side_effects=True, vmem_limit_bytes=VMEM_LIMIT
        ),
        name="gather",
    )(images, w, off)


def features(x):
    wide = x.astype(F32)
    return jnp.concatenate([(wide * wide).astype(BF16), x], axis=1)


def score_kernel(x_ref, w_ref, off_ref, e_ref, peak_ref, lse_ref):
    feats = features(x_ref[...])
    s = lax.dot_general(w_ref[...], feats, (((1,), (1,)), ((), ())), preferred_element_type=F32)
    s = s + off_ref[...]
    peak = jnp.max(s, axis=0, keepdims=True)
    e = jnp.exp(s - peak)
    e_ref[...] = e
    peak_ref[...] = peak
    lse_ref[...] = peak + jnp.log(jnp.sum(e, axis=0, keepdims=True))


def score(x, w, off):
    rows, d = x.shape
    k = w.shape[0]
    n = min(CHUNK, rows)
    whole = lambda i: (0, 0)
    return pl.pallas_call(
        score_kernel,
        grid=(rows // n,),
        out_shape=(
            jax.ShapeDtypeStruct((k, rows), F32),
            jax.ShapeDtypeStruct((1, rows), F32),
            jax.ShapeDtypeStruct((1, rows), F32),
        ),
        in_specs=[
            pl.BlockSpec((n, d), lambda i: (i, 0)),
            pl.BlockSpec((k, 2 * d), whole),
            pl.BlockSpec((k, 1), whole),
        ],
        out_specs=(
            pl.BlockSpec((k, n), lambda i: (0, i)),
            pl.BlockSpec((1, n), lambda i: (0, i)),
            pl.BlockSpec((1, n), lambda i: (0, i)),
        ),
        compiler_params=pltpu.CompilerParams(vmem_limit_bytes=VMEM_LIMIT),
        name="score",
    )(x, w, off)


def lse_kernel(n_mp, lse_ref, peak_ref, logits_ref, factor_ref, like_ref, buf, send, recv):
    a, b, m = lax.axis_index("ca"), lax.axis_index("ib"), lax.axis_index("mp")
    n = SQUARE * n_mp
    me = b * n_mp + m

    def device(k):
        p = lax.rem(me + k, n)
        return (a, p // n_mp, lax.rem(p, n_mp))

    barrier = pltpu.get_barrier_semaphore()

    @pl.loop(1, n)
    def _(k):
        pl.semaphore_signal(barrier, inc=1, device_id=device(k), device_id_type=MESH)

    pl.semaphore_wait(barrier, n - 1)

    def copy(k):
        return remote(lse_ref, buf.at[k], send.at[k], recv.at[k], device(k))

    @pl.loop(1, n)
    def _(k):
        copy(k).start()

    logits = logits_ref[...]
    top = jnp.max(logits, axis=1, keepdims=True)
    logit_total = top + jnp.log(jnp.sum(jnp.exp(logits - top), axis=1, keepdims=True))

    @pl.loop(1, n)
    def _(k):
        copy(k).wait()

    own = lse_ref[...]
    high = lax.fori_loop(1, n, lambda k, h: jnp.maximum(h, buf[k]), own)
    total = lax.fori_loop(1, n, lambda k, t: t + jnp.exp(buf[k] - high), jnp.exp(own - high))
    row_total = high + jnp.log(total)
    factor_ref[...] = jnp.exp(peak_ref[...] - row_total)
    like_ref[...] = row_total - logit_total


def combine(lse, peak, logits, n_mp):
    n = SQUARE * n_mp
    vmem = pl.BlockSpec(memory_space=pltpu.VMEM)
    return pl.pallas_call(
        functools.partial(lse_kernel, n_mp),
        out_shape=(jax.ShapeDtypeStruct(lse.shape, F32),) * 2,
        in_specs=[vmem] * 3,
        out_specs=(vmem,) * 2,
        scratch_shapes=[
            pltpu.VMEM((n,) + lse.shape, F32),
            pltpu.SemaphoreType.DMA((n,)),
            pltpu.SemaphoreType.DMA((n,)),
        ],
        compiler_params=pltpu.CompilerParams(collective_id=1, has_side_effects=True),
        name="combine",
    )(lse, peak, logits[None, :])


def target(k, a, n):
    left, right = a, n - 1 - a
    far, near = jnp.maximum(left, right), jnp.minimum(left, right)
    lead = far - near
    late = jnp.maximum(k - lead, 0)
    dist = jnp.where(k < lead, far - k, near - late // 2)
    to_far = jnp.logical_or(k < lead, lax.rem(late, 2) == 0)
    to_right = jnp.where(right >= left, to_far, jnp.logical_not(to_far))
    return jnp.where(to_right, a + dist, a - dist)


def moment_kernel(n_ca, total, x_ref, e_ref, factor_ref, means_ref, prec_ref,
                  nm_ref, nv_ref, nw_ref, acc, cacc, crow, sbuf, sc, rbuf, rc,
                  msend, mrecv, csend, crecv):
    a, b, m = lax.axis_index("ca"), lax.axis_index("ib"), lax.axis_index("mp")
    k, i = pl.program_id(0), pl.program_id(1)
    last = pl.num_programs(1) - 1
    d = means_ref.shape[1]
    barrier = pltpu.get_barrier_semaphore()

    @pl.when(jnp.logical_and(k == 0, i == 0))
    def _():
        @pl.when(a > 0)
        def _():
            pl.semaphore_signal(barrier, inc=1, device_id=(a - 1, b, m), device_id_type=MESH)

        @pl.when(a < n_ca - 1)
        def _():
            pl.semaphore_signal(barrier, inc=1, device_id=(a + 1, b, m), device_id_type=MESH)

        ends = (a == 0).astype(jnp.int32) + (a == n_ca - 1).astype(jnp.int32)
        pl.semaphore_wait(barrier, 2 - ends)

    def copies(j, way):
        nbr = jnp.clip(a + 1 - 2 * way, 0, n_ca - 1)
        dev = (nbr, b, m)
        return (
            remote(sbuf.at[j], rbuf.at[way, j], msend.at[j], mrecv.at[way, j], dev),
            remote(sc.at[j], rc.at[way, j], csend.at[j], crecv.at[way, j], dev),
        )

    def info(q):
        j = target(q, a, n_ca)
        way = (j < a).astype(jnp.int32)
        joined = jnp.where(j < a, a < n_ca - 1, a > 0)
        return j, way, joined

    def start(q):
        j, way, _ = info(q)
        for c in copies(j, way):
            c.start()

    def merge(q):
        j, way, _ = info(q)
        for c in copies(j, way):
            c.wait_recv()
        sbuf[j] = (acc[q] + rbuf[way, j].astype(F32)).astype(BF16)
        sc[j] = crow[q] + rc[way, j]

    @pl.when(jnp.logical_and(i == 0, k >= 1))
    def _():
        @pl.when(jnp.logical_not(info(k - 1)[2]))
        def _():
            start(k - 1)

        @pl.when(jnp.logical_and(k >= 2, info(jnp.maximum(k - 2, 0))[2]))
        def _():
            start(k - 2)

    feats = features(x_ref[...])
    shares = (e_ref[...] * factor_ref[...]).astype(BF16)
    wide = shares.astype(F32)
    part = wide[:, :128]
    for q in range(1, wide.shape[1] // 128):
        part = part + wide[:, q * 128:(q + 1) * 128]
    prod = jnp.dot(shares, feats, preferred_element_type=F32)

    @pl.when(i == 0)
    def _():
        acc[k] = prod
        cacc[...] = part

    @pl.when(i > 0)
    def _():
        acc[k] += prod
        cacc[...] += part

    @pl.when(i == last)
    def _():
        crow[k] = jnp.sum(cacc[...].T, axis=0, keepdims=True)

        @pl.when(jnp.logical_and(k < n_ca - 1, jnp.logical_not(info(k)[2])))
        def _():
            j = info(k)[0]
            sbuf[j] = acc[k].astype(BF16)
            sc[j] = crow[k]

        @pl.when(jnp.logical_and(k >= 1, info(jnp.maximum(k - 1, 0))[2]))
        def _():
            merge(k - 1)

        @pl.when(k == n_ca - 1)
        def _():
            means, prec = means_ref[...], prec_ref[...]
            nm_ref[...] = acc[n_ca - 1, :, d:] + means
            nv_ref[...] = acc[n_ca - 1, :, :d] + 1.0 / prec + means * means

            @pl.when(info(n_ca - 2)[2])
            def _():
                start(n_ca - 2)

            def join(way):
                for c in copies(a, way):
                    c.wait_recv()
                nm_ref[...] += rbuf[way, a, :, d:].astype(F32)
                nv_ref[...] += rbuf[way, a, :, :d].astype(F32)
                crow[n_ca - 1] += rc[way, a]

            @pl.when(a > 0)
            def _():
                join(0)

            @pl.when(a < n_ca - 1)
            def _():
                join(1)

            denominator = crow[n_ca - 1] + 1.0
            nw_ref[...] = jnp.log(denominator) - jnp.log(jnp.full_like(denominator, total))
            rows = denominator.shape[1]
            column = jnp.broadcast_to(denominator, (128, rows)).T
            wide_column = jnp.concatenate([column] * (d // 128), axis=1)
            new_means = nm_ref[...] / wide_column
            nm_ref[...] = new_means
            nv_ref[...] = nv_ref[...] / wide_column - new_means * new_means

            @pl.loop(0, n_ca - 1)
            def _(q):
                j, way, _ = info(q)
                for c in copies(j, way):
                    c.wait_send()


def moment(x, e, factor, means, precisions, n_ca, total):
    rows, d = x.shape
    r = means.shape[0]
    n = min(2048, rows)
    dma = pltpu.SemaphoreType.DMA
    fixed = lambda k, i: (0, 0)

    def e_map(k, i):
        return target(k, lax.axis_index("ca"), n_ca), i

    return pl.pallas_call(
        functools.partial(moment_kernel, n_ca, total),
        grid=(n_ca, rows // n),
        out_shape=(
            jax.ShapeDtypeStruct((r, d), F32),
            jax.ShapeDtypeStruct((r, d), F32),
            jax.ShapeDtypeStruct((1, r), F32),
        ),
        in_specs=[
            pl.BlockSpec((n, d), lambda k, i: (i, 0)),
            pl.BlockSpec((r, n), e_map),
            pl.BlockSpec((1, n), lambda k, i: (0, i)),
            pl.BlockSpec((r, d), fixed),
            pl.BlockSpec((r, d), fixed),
        ],
        out_specs=(
            pl.BlockSpec((r, d), fixed),
            pl.BlockSpec((r, d), fixed),
            pl.BlockSpec((1, r), fixed),
        ),
        scratch_shapes=[
            pltpu.VMEM((n_ca, r, 2 * d), F32),
            pltpu.VMEM((r, 128), F32),
            pltpu.VMEM((n_ca, 1, r), F32),
            pltpu.VMEM((n_ca, r, 2 * d), BF16),
            pltpu.VMEM((n_ca, 1, r), F32),
            pltpu.VMEM((2, n_ca, r, 2 * d), BF16),
            pltpu.VMEM((2, n_ca, 1, r), F32),
            dma((n_ca,)),
            dma((2, n_ca)),
            dma((n_ca,)),
            dma((2, n_ca)),
        ],
        compiler_params=pltpu.CompilerParams(
            collective_id=2, has_side_effects=True, vmem_limit_bytes=VMEM_LIMIT
        ),
        name="moment",
    )(x, e, factor, means, precisions)


def body(n_ca, n_mp, images, means, precisions, logits):
    t, d = images.shape
    r = means.shape[0]
    a, b, m = lax.axis_index("ca"), lax.axis_index("ib"), lax.axis_index("mp")
    own_logits = lax.dynamic_slice_in_dim(logits, ((m * n_ca + a) * SQUARE + b) * r, r)
    prec_b = precisions.astype(BF16)
    w = jnp.concatenate([-0.5 * prec_b, (means * precisions).astype(BF16)], axis=1)
    off = (
        own_logits
        + 0.5 * jnp.sum(jnp.log(precisions) - means * means * precisions, axis=1)
        - 0.5 * d * math.log(2.0 * math.pi)
    )
    imgs, w_all, off_all = gather(images, w, off[None, :], n_ca)
    x = imgs.reshape(SQUARE * t, d)
    e, peak, lse = score(x, w_all.reshape(n_ca * r, 2 * d), off_all.reshape(n_ca * r, 1))
    factor, like = combine(lse, peak, logits, n_mp)
    log_likelihood = lax.dynamic_slice_in_dim(like[0], b * t, t)
    total = float(t * n_ca * SQUARE + logits.shape[0])
    new_means, new_variances, weights = moment(x, e, factor, means, precisions, n_ca, total)
    return (new_means, new_variances, weights[0], log_likelihood)


def solution(mesh):
    n_dp, n_mp = mesh.shape["dp"], mesh.shape["mp"]
    n_ca = n_dp // SQUARE
    split = Mesh(mesh.devices.reshape(n_ca, SQUARE, n_mp), ("ca", "ib", "mp"))
    dp = ("ca", "ib")
    comp = ("mp", "ca", "ib")
    return jax.shard_map(
        functools.partial(body, n_ca, n_mp),
        mesh=split,
        in_specs=(P(dp, None), P(comp, None), P(comp, None), P()),
        out_specs=(P(comp, None), P(comp, None), P(comp), P(dp)),
        check_vma=False,
    )
```

```python
import functools
import math

import jax
import jax.numpy as jnp
from jax import lax
from jax.experimental import pallas as pl
from jax.experimental.pallas import tpu as pltpu
from jax.sharding import Mesh, PartitionSpec as P

MESH = pl.DeviceIdType.MESH
SQUARE = 4
PIECES = 2
F32 = jnp.float32
BF16 = jnp.bfloat16
VMEM_LIMIT = 60 * 1024 * 1024


def remote(src, dst, send, recv, device):
    return pltpu.make_async_remote_copy(
        src_ref=src, dst_ref=dst, send_sem=send, recv_sem=recv, device_id=device, device_id_type=MESH
    )


def features(x):
    wide = x.astype(F32)
    return jnp.concatenate([(wide * wide).astype(BF16), x], axis=1)


def target(k, a, n):
    left, right = a, n - 1 - a
    far, near = jnp.maximum(left, right), jnp.minimum(left, right)
    lead = far - near
    late = jnp.maximum(k - lead, 0)
    dist = jnp.where(k < lead, far - k, near - late // 2)
    to_far = jnp.logical_or(k < lead, lax.rem(late, 2) == 0)
    to_right = jnp.where(right >= left, to_far, jnp.logical_not(to_far))
    return jnp.where(to_right, a + dist, a - dist)


def score_kernel(n_ca, img_ref, w_ref, off_ref, imgs_out, e_out, peak_ref, lse_ref,
                 imgs, wall, offall, ebuf, blk_lse, loc, isend, irecv,
                 wsend, wrecv, osend, orecv, esem, psem):
    a, b, m = lax.axis_index("ca"), lax.axis_index("ib"), lax.axis_index("mp")
    t_rows = img_ref.shape[0]
    r = w_ref.shape[0]
    core = lax.rem(m, 2)
    partner = m + 1 - 2 * core
    bx = b + 1 - 2 * lax.rem(b, 2)
    by = lax.rem(b + 2, 4)
    bd = lax.rem(bx + 2, 4)
    to_x, to_y, to_p = (a, bx, m), (a, by, m), (a, b, partner)
    sub = t_rows // (2 * PIECES)

    barrier = pltpu.get_barrier_semaphore()
    for dev in (to_x, to_y, to_p):
        pl.semaphore_signal(barrier, inc=1, device_id=dev, device_id_type=MESH)

    @pl.when(a > 0)
    def _():
        pl.semaphore_signal(barrier, inc=1, device_id=(a - 1, b, m), device_id_type=MESH)

    @pl.when(a < n_ca - 1)
    def _():
        pl.semaphore_signal(barrier, inc=1, device_id=(a + 1, b, m), device_id_type=MESH)

    own = (
        pltpu.make_async_copy(img_ref, imgs.at[b], loc.at[0]),
        pltpu.make_async_copy(w_ref, wall.at[a], loc.at[1]),
        pltpu.make_async_copy(off_ref, offall.at[a], loc.at[2]),
    )
    for c in own:
        c.start()
    ends = (a == 0).astype(jnp.int32) + (a == n_ca - 1).astype(jnp.int32)
    pl.semaphore_wait(barrier, 5 - ends)

    def img_copy(k, i, dev, piece, first=False):
        rows = pl.ds(pl.multiple_of((core * PIECES + piece) * sub, sub), sub)
        dst = imgs.at[i, rows]
        return remote(img_ref.at[rows] if first else dst, dst, isend.at[k, piece], irecv.at[k, piece], dev)

    def chain(way, s, blk, first=False):
        blk = jnp.clip(blk, 0, n_ca - 1)
        dev = (jnp.clip(a + 1 - 2 * way, 0, n_ca - 1), b, m)
        return (
            remote(w_ref if first else wall.at[blk], wall.at[blk], wsend.at[way, s], wrecv.at[way, s], dev),
            remote(off_ref if first else offall.at[blk], offall.at[blk], osend.at[way, s], orecv.at[way, s], dev),
        )

    def has_next(way):
        return jnp.where(way == 0, a < n_ca - 1, a > 0)

    for way in (0, 1):
        @pl.when(has_next(way))
        def _():
            for c in chain(way, 0, a, True):
                c.start()

    for piece in range(PIECES):
        img_copy(0, b, to_x, piece, True).start()
        img_copy(1, b, to_y, piece, True).start()
    for c in own:
        c.wait()

    def place(q):
        j = target(n_ca - 1 - q, a, n_ca)
        return j, (j > a).astype(jnp.int32)

    def take(q):
        j, way = place(q)
        s = jnp.maximum(jnp.abs(a - j) - 1, 0)
        for c in chain(way, s, j):
            c.wait_recv()

        @pl.when(has_next(way))
        def _():
            for c in chain(way, s + 1, j):
                c.start()

    def images_in(piece):
        img_copy(0, bx, to_x, piece).wait_recv()
        img_copy(3, bx, to_p, piece).start()

        @pl.when(core == 0)
        def _():
            img_copy(2, bx, to_y, piece).start()

        img_copy(1, by, to_y, piece).wait_recv()
        img_copy(4, by, to_p, piece).start()

        @pl.when(core == 1)
        def _():
            img_copy(2, by, to_x, piece).start()

    def corner_in(piece):
        img_copy(2, bd, to_x, piece).wait_recv()
        img_copy(5, bd, to_p, piece).start()

    def paired(k, i):
        for piece in range(PIECES):
            img_copy(k, i, to_p, piece).wait_recv()

    def put(i, slot):
        return pltpu.make_async_copy(imgs.at[i], imgs_out.at[i], psem.at[slot])

    def shard(p):
        return jnp.where(p == 0, b, jnp.where(p == 1, bx, jnp.where(p == 2, by, bd)))

    near = n_ca - 1

    def e_copy(t, j, i):
        slot = lax.rem(t, 2)
        rows = pl.ds(pl.multiple_of(j * r, r), r)
        cols = pl.ds(pl.multiple_of(i * t_rows, t_rows), t_rows)
        return pltpu.make_async_copy(ebuf.at[slot], e_out.at[rows, cols], esem.at[slot])

    @pl.loop(0, 4 * n_ca)
    def _(t):
        p = jnp.where(t < 3 * near, t // near, jnp.where(t < 3 * n_ca, t - 3 * near, 3))
        q = jnp.where(t < 3 * near, lax.rem(t, near), jnp.where(t < 3 * n_ca, near, t - 3 * n_ca))

        @pl.when(t == near - 1)
        def _():
            for piece in range(PIECES - 1):
                images_in(piece)

        @pl.when(jnp.logical_and(t >= 1, t < near))
        def _():
            take(jnp.clip(t, 1, near))

        @pl.when(t == near)
        def _():
            put(b, 0).start()
            images_in(PIECES - 1)

            @pl.when(has_next(place(near)[1]))
            def _():
                take(near)

            paired(3, bx)

        @pl.when(t == 2 * near)
        def _():
            put(bx, 1).start()
            for piece in range(PIECES - 1):
                corner_in(piece)
            paired(4, by)

        @pl.when(t == 3 * near)
        def _():
            put(by, 2).start()
            corner_in(PIECES - 1)

            @pl.when(jnp.logical_not(has_next(place(near)[1])))
            def _():
                take(near)

        @pl.when(t == 3 * n_ca)
        def _():
            paired(5, bd)
            put(bd, 3).start()

        i = shard(p)
        j = place(q)[0]

        @pl.when(t >= 2)
        def _():
            e_copy(t, j, i).wait()

        cols = pl.ds(pl.multiple_of(i * t_rows, t_rows), t_rows)
        feats = features(imgs[i])
        s = lax.dot_general(wall[j], feats, (((1,), (1,)), ((), ())), preferred_element_type=F32)
        column = jnp.broadcast_to(offall[j], (128, r)).T
        s = s + column[:, :1]
        peak = jnp.max(s, axis=0, keepdims=True)
        e = jnp.exp(s - peak)
        ebuf[lax.rem(t, 2)] = e
        peak_ref[j, :, cols] = peak
        blk_lse[j, :, cols] = peak + jnp.log(jnp.sum(e, axis=0, keepdims=True))
        e_copy(t, j, i).start()

    high = lax.fori_loop(1, n_ca, lambda k, h: jnp.maximum(h, blk_lse[k]), blk_lse[0])
    tot = lax.fori_loop(1, n_ca, lambda k, x: x + jnp.exp(blk_lse[k] - high), jnp.exp(blk_lse[0] - high))
    lse_ref[...] = high + jnp.log(tot)

    for t in (0, 1):
        e_copy(t, a, b).wait()
    for slot, i in enumerate((b, bx, by, bd)):
        put(i, slot).wait()
    for k, i in enumerate((b, b, bd, bx, by, bd)):
        for piece in range(PIECES):
            img_copy(k, i, to_p, piece).wait_send()
    for way in (0, 1):
        @pl.loop(0, n_ca - 1)
        def _(s):
            blk = a - s + 2 * way * s
            ok = jnp.logical_and(has_next(way), jnp.logical_and(blk >= 0, blk < n_ca))

            @pl.when(ok)
            def _():
                for c in chain(way, s, blk):
                    c.wait_send()


def score(images, w, off, n_ca):
    t, d = images.shape
    r = w.shape[0]
    rows = SQUARE * t
    any_spec = pl.BlockSpec(memory_space=pl.ANY)
    vmem = pl.BlockSpec(memory_space=pltpu.VMEM)
    dma = pltpu.SemaphoreType.DMA
    line = dma((2, n_ca - 1))
    return pl.pallas_call(
        functools.partial(score_kernel, n_ca),
        out_shape=(
            jax.ShapeDtypeStruct((SQUARE, t, d), BF16),
            jax.ShapeDtypeStruct((n_ca * r, rows), F32),
            jax.ShapeDtypeStruct((n_ca, 1, rows), F32),
            jax.ShapeDtypeStruct((1, rows), F32),
        ),
        in_specs=[any_spec, vmem, vmem],
        out_specs=(any_spec, any_spec, vmem, vmem),
        scratch_shapes=[
            pltpu.VMEM((SQUARE, t, d), BF16),
            pltpu.VMEM((n_ca, r, 2 * d), BF16),
            pltpu.VMEM((n_ca, 1, r), F32),
            pltpu.VMEM((2, r, t), F32),
            pltpu.VMEM((n_ca, 1, rows), F32),
            dma((3,)),
            dma((6, PIECES)),
            dma((6, PIECES)),
            line, line, line, line,
            dma((2,)),
            dma((4,)),
        ],
        compiler_params=pltpu.CompilerParams(
            collective_id=0, has_side_effects=True, vmem_limit_bytes=VMEM_LIMIT
        ),
        name="score",
    )(images, w, off)


def lse_kernel(n_mp, lse_ref, peak_ref, logits_ref, factor_ref, like_ref, buf, send, recv):
    a, b, m = lax.axis_index("ca"), lax.axis_index("ib"), lax.axis_index("mp")
    n = SQUARE * n_mp
    me = b * n_mp + m

    def device(k):
        p = lax.rem(me + k, n)
        return (a, p // n_mp, lax.rem(p, n_mp))

    barrier = pltpu.get_barrier_semaphore()

    @pl.loop(1, n)
    def _(k):
        pl.semaphore_signal(barrier, inc=1, device_id=device(k), device_id_type=MESH)

    pl.semaphore_wait(barrier, n - 1)

    def copy(k):
        return remote(lse_ref, buf.at[k], send.at[k], recv.at[k], device(k))

    @pl.loop(1, n)
    def _(k):
        copy(k).start()

    logits = logits_ref[...]
    top = jnp.max(logits, axis=1, keepdims=True)
    logit_total = top + jnp.log(jnp.sum(jnp.exp(logits - top), axis=1, keepdims=True))

    @pl.loop(1, n)
    def _(k):
        copy(k).wait()

    own = lse_ref[...]
    high = lax.fori_loop(1, n, lambda k, h: jnp.maximum(h, buf[k]), own)
    total = lax.fori_loop(1, n, lambda k, t: t + jnp.exp(buf[k] - high), jnp.exp(own - high))
    row_total = high + jnp.log(total)
    factor_ref[...] = jnp.exp(peak_ref[...] - row_total[None])
    like_ref[...] = row_total - logit_total


def combine(lse, peak, logits, n_mp):
    n = SQUARE * n_mp
    vmem = pl.BlockSpec(memory_space=pltpu.VMEM)
    return pl.pallas_call(
        functools.partial(lse_kernel, n_mp),
        out_shape=(jax.ShapeDtypeStruct(peak.shape, F32), jax.ShapeDtypeStruct(lse.shape, F32)),
        in_specs=[vmem] * 3,
        out_specs=(vmem,) * 2,
        scratch_shapes=[
            pltpu.VMEM((n,) + lse.shape, F32),
            pltpu.SemaphoreType.DMA((n,)),
            pltpu.SemaphoreType.DMA((n,)),
        ],
        compiler_params=pltpu.CompilerParams(collective_id=1, has_side_effects=True),
        name="combine",
    )(lse, peak, logits[None, :])


def moment_kernel(n_ca, total, x_ref, e_ref, factor_ref, means_ref, prec_ref,
                  nm_ref, nv_ref, nw_ref, acc, cacc, crow, sbuf, sc, rbuf, rc,
                  msend, mrecv, csend, crecv):
    a, b, m = lax.axis_index("ca"), lax.axis_index("ib"), lax.axis_index("mp")
    k, i = pl.program_id(0), pl.program_id(1)
    last = pl.num_programs(1) - 1
    d = means_ref.shape[1]
    barrier = pltpu.get_barrier_semaphore()

    @pl.when(jnp.logical_and(k == 0, i == 0))
    def _():
        @pl.when(a > 0)
        def _():
            pl.semaphore_signal(barrier, inc=1, device_id=(a - 1, b, m), device_id_type=MESH)

        @pl.when(a < n_ca - 1)
        def _():
            pl.semaphore_signal(barrier, inc=1, device_id=(a + 1, b, m), device_id_type=MESH)

        ends = (a == 0).astype(jnp.int32) + (a == n_ca - 1).astype(jnp.int32)
        pl.semaphore_wait(barrier, 2 - ends)

    def copies(j, way):
        nbr = jnp.clip(a + 1 - 2 * way, 0, n_ca - 1)
        dev = (nbr, b, m)
        return (
            remote(sbuf.at[j], rbuf.at[way, j], msend.at[j], mrecv.at[way, j], dev),
            remote(sc.at[j], rc.at[way, j], csend.at[j], crecv.at[way, j], dev),
        )

    def info(q):
        j = target(q, a, n_ca)
        way = (j < a).astype(jnp.int32)
        joined = jnp.where(j < a, a < n_ca - 1, a > 0)
        return j, way, joined

    def start(q):
        j, way, _ = info(q)
        for c in copies(j, way):
            c.start()

    def merge(q):
        j, way, _ = info(q)
        for c in copies(j, way):
            c.wait_recv()
        sbuf[j] = (acc[q] + rbuf[way, j].astype(F32)).astype(BF16)
        sc[j] = crow[q] + rc[way, j]

    @pl.when(jnp.logical_and(i == 0, k >= 1))
    def _():
        @pl.when(jnp.logical_not(info(k - 1)[2]))
        def _():
            start(k - 1)

        @pl.when(jnp.logical_and(k >= 2, info(jnp.maximum(k - 2, 0))[2]))
        def _():
            start(k - 2)

    feats = features(x_ref[...])
    shares = (e_ref[...] * factor_ref[0]).astype(BF16)
    wide = shares.astype(F32)
    part = wide[:, :128]
    for q in range(1, wide.shape[1] // 128):
        part = part + wide[:, q * 128:(q + 1) * 128]
    prod = jnp.dot(shares, feats, preferred_element_type=F32)

    @pl.when(i == 0)
    def _():
        acc[k] = prod
        cacc[...] = part

    @pl.when(i > 0)
    def _():
        acc[k] += prod
        cacc[...] += part

    @pl.when(i == last)
    def _():
        crow[k] = jnp.sum(cacc[...].T, axis=0, keepdims=True)

        @pl.when(jnp.logical_and(k < n_ca - 1, jnp.logical_not(info(k)[2])))
        def _():
            j = info(k)[0]
            sbuf[j] = acc[k].astype(BF16)
            sc[j] = crow[k]

        @pl.when(jnp.logical_and(k >= 1, info(jnp.maximum(k - 1, 0))[2]))
        def _():
            merge(k - 1)

        @pl.when(k == n_ca - 1)
        def _():
            means, prec = means_ref[...], prec_ref[...]
            nm_ref[...] = acc[n_ca - 1, :, d:] + means
            nv_ref[...] = acc[n_ca - 1, :, :d] + 1.0 / prec + means * means

            @pl.when(info(n_ca - 2)[2])
            def _():
                start(n_ca - 2)

            def join(way):
                for c in copies(a, way):
                    c.wait_recv()
                nm_ref[...] += rbuf[way, a, :, d:].astype(F32)
                nv_ref[...] += rbuf[way, a, :, :d].astype(F32)
                crow[n_ca - 1] += rc[way, a]

            @pl.when(a > 0)
            def _():
                join(0)

            @pl.when(a < n_ca - 1)
            def _():
                join(1)

            denominator = crow[n_ca - 1] + 1.0
            nw_ref[...] = jnp.log(denominator) - jnp.log(jnp.full_like(denominator, total))
            rows = denominator.shape[1]
            column = jnp.broadcast_to(denominator, (128, rows)).T
            wide_column = jnp.concatenate([column] * (d // 128), axis=1)
            new_means = nm_ref[...] / wide_column
            nm_ref[...] = new_means
            nv_ref[...] = nv_ref[...] / wide_column - new_means * new_means

            @pl.loop(0, n_ca - 1)
            def _(q):
                j, way, _ = info(q)
                for c in copies(j, way):
                    c.wait_send()


def moment(x, e, factor, means, precisions, n_ca, total):
    rows, d = x.shape
    r = means.shape[0]
    n = min(2048, rows)
    dma = pltpu.SemaphoreType.DMA
    fixed = lambda k, i: (0, 0)

    def e_map(k, i):
        return target(k, lax.axis_index("ca"), n_ca), i

    def f_map(k, i):
        return target(k, lax.axis_index("ca"), n_ca), 0, i

    return pl.pallas_call(
        functools.partial(moment_kernel, n_ca, total),
        grid=(n_ca, rows // n),
        out_shape=(
            jax.ShapeDtypeStruct((r, d), F32),
            jax.ShapeDtypeStruct((r, d), F32),
            jax.ShapeDtypeStruct((1, r), F32),
        ),
        in_specs=[
            pl.BlockSpec((n, d), lambda k, i: (i, 0)),
            pl.BlockSpec((r, n), e_map),
            pl.BlockSpec((1, 1, n), f_map),
            pl.BlockSpec((r, d), fixed),
            pl.BlockSpec((r, d), fixed),
        ],
        out_specs=(
            pl.BlockSpec((r, d), fixed),
            pl.BlockSpec((r, d), fixed),
            pl.BlockSpec((1, r), fixed),
        ),
        scratch_shapes=[
            pltpu.VMEM((n_ca, r, 2 * d), F32),
            pltpu.VMEM((r, 128), F32),
            pltpu.VMEM((n_ca, 1, r), F32),
            pltpu.VMEM((n_ca, r, 2 * d), BF16),
            pltpu.VMEM((n_ca, 1, r), F32),
            pltpu.VMEM((2, n_ca, r, 2 * d), BF16),
            pltpu.VMEM((2, n_ca, 1, r), F32),
            dma((n_ca,)),
            dma((2, n_ca)),
            dma((n_ca,)),
            dma((2, n_ca)),
        ],
        compiler_params=pltpu.CompilerParams(
            collective_id=2, has_side_effects=True, vmem_limit_bytes=VMEM_LIMIT
        ),
        name="moment",
    )(x, e, factor, means, precisions)


def body(n_ca, n_mp, images, means, precisions, logits):
    t, d = images.shape
    r = means.shape[0]
    a, b, m = lax.axis_index("ca"), lax.axis_index("ib"), lax.axis_index("mp")
    own_logits = lax.dynamic_slice_in_dim(logits, ((m * n_ca + a) * SQUARE + b) * r, r)
    prec_b = precisions.astype(BF16)
    w = jnp.concatenate([-0.5 * prec_b, (means * precisions).astype(BF16)], axis=1)
    off = (
        own_logits
        + 0.5 * jnp.sum(jnp.log(precisions) - means * means * precisions, axis=1)
        - 0.5 * d * math.log(2.0 * math.pi)
    )
    imgs, e, peak, lse = score(images, w, off[None, :], n_ca)
    x = imgs.reshape(SQUARE * t, d)
    factor, like = combine(lse, peak, logits, n_mp)
    log_likelihood = lax.dynamic_slice_in_dim(like[0], b * t, t)
    total = float(t * n_ca * SQUARE + logits.shape[0])
    new_means, new_variances, weights = moment(x, e, factor, means, precisions, n_ca, total)
    return (new_means, new_variances, weights[0], log_likelihood)


def solution(mesh):
    n_dp, n_mp = mesh.shape["dp"], mesh.shape["mp"]
    n_ca = n_dp // SQUARE
    split = Mesh(mesh.devices.reshape(n_ca, SQUARE, n_mp), ("ca", "ib", "mp"))
    dp = ("ca", "ib")
    comp = ("mp", "ca", "ib")
    return jax.shard_map(
        functools.partial(body, n_ca, n_mp),
        mesh=split,
        in_specs=(P(dp, None), P(comp, None), P(comp, None), P()),
        out_specs=(P(comp, None), P(comp, None), P(comp), P(dp)),
        check_vma=False,
    )
```
